32 devices in a mesh: group: 2 (over y), user: 2 (over core), cand: 8 (over z, x).
Axes of the slice: x: 2, y: 2, z: 4, core: 2. Of those that a mesh axis runs over, the one named last changes fastest.
Arguments:
- history: bfloat16 [4, 1024, 1024], P(('group', 'user'), None, 'cand'), parts along dimension 0, may hold values from -6 to 6
- hist_len: int32 [4], P(('group', 'user')), parts along dimension 0, may hold values from 256 to 1024
- tile_counts: int32 [4, 8], P(('group', 'user'), 'cand'), parts along dimension 0, may hold values from 0 to 3, as said below
- cand_emb: bfloat16 [4, 3072, 1024], P(('group', 'user'), 'cand'), parts along dimension 0, may hold values from -3 to 3
- w_in: bfloat16 [1024, 4096], P(None, 'cand'), may hold values from -1 to 1
- out_gain: float32 [1024], replicated, may hold values from 0.25 to 1.75
- w_out: bfloat16 [1024, 1024], P(None, 'cand'), may hold values from -0.1875 to 0.1875
Outputs:
- cand_out: bfloat16 [4, 3072, 1024], P(('group', 'user'), 'cand'), parts along dimension 0
The draws below stay inside these ranges and needn't reach their ends.
There are 2 independent parts, one for each index of `group`. The reference program is written for one: setup_inputs(seed, part) draws one part's arguments, and reference() takes and returns one part's arrays. A program takes and returns all parts, laid end to end along the dimension named above; an argument that names none is the same for every part. Nothing has to cross between parts.
Inputs may be any that keep to these rules, and one draw needn't show every extreme that they name: In each user's row of tile_counts exactly 1 entries equal 3, 2 * (1) entries are 0 and all others are 1, so that each row sums to its number of entries; which entries take which value is random.
All inputs are finite; a program needn't handle non-finite values.
Results may differ from the reference program's by a relative error of at most 0.0069.
Values may be sent and summed in bfloat16 or wider, within the bound.
A program may use at most 64 MiB of HBM per device.

```python
import math
import jax
import jax.numpy as jnp
from jax import lax

D = 1024
HEADS = 8
DH = 128
HIST = 1024
TILE = 128
CAP = 3
USERS = 2
SLOTS = 3072
N_CAND = 8


def draw_tile_counts(key, part):
    row_keys = jax.random.split(key, USERS)
    heavy = N_CAND // 8
    index_row = jnp.arange(N_CAND, dtype=jnp.int32)
    pattern = jnp.where(index_row < heavy, CAP, jnp.where(index_row < CAP * heavy, 0, 1)).astype(jnp.int32)

    def one_row(row_key):
        order = jax.random.permutation(row_key, N_CAND)
        return jnp.take(pattern, order)
    return jax.vmap(one_row)(row_keys).astype(jnp.int32)


def unit_entries(key, shape):
    return jnp.clip(jax.random.normal(key, shape, jnp.float32), -6.0, 6.0)


def draw_w_in(key, part):
    base_key = jax.random.fold_in(key, 11)
    extra_key = jax.random.fold_in(key, 12)
    mix_key = jax.random.fold_in(key, 13)
    base = unit_entries(base_key, (D, 4 * D))
    extra = unit_entries(extra_key, (D, D))
    head_mix = jax.random.uniform(mix_key, (HEADS,), jnp.float32, 0.6, 0.9)
    column_mix = jnp.repeat(head_mix, DH)[None, :]
    query_part = base[:, 2 * D:3 * D]
    key_part = column_mix * query_part + jnp.sqrt(1.0 - column_mix * column_mix) * extra
    whole = jnp.concatenate([base[:, :3 * D], key_part], axis=1) * D ** (-0.5)
    return jnp.clip(whole, -1.0, 1.0).astype(jnp.bfloat16)


def level_of(own_key, dims, cuts, least, top_value):
    level = 1.0
    for position, blocks in cuts:
        steps = jax.random.uniform(jax.random.fold_in(jax.random.fold_in(own_key, 6), position), (blocks,), jnp.float32, least / len(cuts), top_value / len(cuts))
        level = level * jnp.repeat(jnp.exp(steps), dims[position] // blocks).reshape((-1,) + (1,) * (len(dims) - 1 - position))
    return level


def gaussian(stream_key, extent, scale, most, shards=(), kind=jnp.bfloat16):
    drawn = scale * jax.random.normal(stream_key, extent, jnp.float32)
    if shards:
        drawn = drawn * level_of(stream_key, extent, shards, -0.22, 0.18)
    return jnp.clip(drawn, -most, most).astype(kind)


def setup_inputs(seed: int = 0, part: int = 0) -> dict:
    streams_of = jax.random.split(jax.random.key(seed), 8)
    part_splits = jax.random.split(jax.random.fold_in(streams_of[7], part), 8)
    return {
        "history": gaussian(part_splits[0], (USERS, HIST, D), 1.0, 6.0, ((0, 2), (2, 8))),
        "hist_len": jax.random.randint(part_splits[1], (USERS,), HIST // 4, HIST + 1).astype(jnp.int32),
        "tile_counts": draw_tile_counts(jax.random.fold_in(jax.random.fold_in(streams_of[7], part), 71), part),
        "cand_emb": gaussian(part_splits[3], (USERS, SLOTS, D), 0.5, 3.0, ((0, 2), (1, 8))),
        "w_in": draw_w_in(jax.random.fold_in(streams_of[7], 71), part),
        "out_gain": jnp.clip(1.0 + 0.15 * jax.random.normal(streams_of[5], (D,), jnp.float32), 0.25, 1.75),
        "w_out": gaussian(streams_of[6], (D, D), D ** -0.5, 0.1875, ((1, 8),)),
    }


def layer_norm(values):
    center = values - lax.optimization_barrier(jnp.mean(values, axis=-1, keepdims=True))
    spread = lax.optimization_barrier(jnp.mean(center * center, axis=-1, keepdims=True))
    return center * lax.rsqrt(spread + 1e-05)

def reference(history, hist_len, tile_counts, cand_emb, w_in, out_gain, w_out):
    score_scale = 1.0 / math.sqrt(DH)
    kv_weights = jnp.concatenate([w_in[:, D:2 * D], w_in[:, 3 * D:]], axis=1)
    results = []
    for user_row in range(USERS):
        hist_normed = layer_norm(history[user_row].astype(jnp.float32)).astype(jnp.bfloat16)
        hist_kv = jax.nn.silu(jnp.dot(hist_normed, kv_weights, preferred_element_type=jnp.float32)).astype(jnp.bfloat16)
        hist_values = hist_kv[:, :D].reshape(HIST, HEADS, DH).astype(jnp.float32)
        hist_keys = hist_kv[:, D:].reshape(HIST, HEADS, DH).astype(jnp.float32)
        keep_keys = jnp.arange(HIST, dtype=jnp.int32) < hist_len[user_row]
        emb_blocks = cand_emb[user_row].reshape(N_CAND, CAP * TILE, D)

        def score_block(block_args):
            embedded, block_count = block_args
            normed = layer_norm(embedded.astype(jnp.float32)).astype(jnp.bfloat16)
            proj = jax.nn.silu(jnp.dot(normed, w_in, preferred_element_type=jnp.float32)).astype(jnp.bfloat16)
            rows_here = proj.shape[0]
            gate_part = proj[:, :D].astype(jnp.float32)
            cand_values = proj[:, D:2 * D].reshape(rows_here, HEADS, DH).astype(jnp.float32)
            queries = proj[:, 2 * D:3 * D].reshape(rows_here, HEADS, DH).astype(jnp.float32)
            cand_keys = proj[:, 3 * D:].reshape(rows_here, HEADS, DH).astype(jnp.float32)
            scores = jnp.einsum('rhe,the->hrt', queries, hist_keys) * score_scale
            attn_weights = jnp.where(keep_keys[None, None, :], jax.nn.silu(scores), 0.0).astype(jnp.bfloat16)
            attn = jnp.einsum('hrt,the->rhe', attn_weights.astype(jnp.float32), hist_values)
            own_score = jax.nn.silu(lax.optimization_barrier(jnp.sum(queries * cand_keys, axis=-1)) * score_scale)
            attn = (attn + own_score[:, :, None] * cand_values).reshape(rows_here, D)
            gated = (layer_norm(attn) * out_gain[None, :] * gate_part).astype(jnp.bfloat16)
            output = embedded.astype(jnp.float32) + jnp.dot(gated, w_out, preferred_element_type=jnp.float32)
            live = jnp.arange(rows_here, dtype=jnp.int32) < block_count * TILE
            return jnp.where(live[:, None], output, 0.0).astype(jnp.bfloat16)
        scored = lax.map(score_block, (emb_blocks, tile_counts[user_row]))
        results.append(scored.reshape(SLOTS, D))
    return jnp.stack(results)
```

```python
import functools
import math

import jax
import jax.numpy as jnp
from jax import lax
from jax.experimental import pallas as pl
from jax.experimental.pallas import tpu as pltpu
from jax.sharding import PartitionSpec as P

D = 1024
HEADS = 8
DH = 128
TILE = 128
RING = 8
MESH = pl.DeviceIdType.MESH


def layer_norm(values, scale=1.0):
    center = values - jnp.mean(values, axis=-1, keepdims=True)
    spread = jnp.mean(center * center, axis=-1, keepdims=True)
    return center * (lax.rsqrt(spread + 1e-05) * scale)


def half_silu(half):
    return half + half * jnp.tanh(half)


def cand_of(place):
    high = place // 4
    return (1 - high) * (2 * place) + high * (15 - 2 * place)


def place_of(cand):
    row, column = cand // 2, cand % 2
    return (1 - column) * row + column * (7 - row)


PIECES = (4, 2, 2)
O_PARTS = 2

PLAN = (
    ('send', 'W0'),
    ('send', 'H2'),
    ('send', 'H1'),
    ('nb',),
    ('pc', 'W0', 'own'),
    ('pc', 'W1', 'own'),
    ('ring', 'W0', 0),
    ('send', 'H0'),
    ('ring', 'H2', 0),
    ('ring', 'H1', 0),
    ('ring', 'W0', 1),
    ('side', 'W0', 0),
    ('ring', 'H0', 0),
    ('send', 'W1'),
    ('full', 'W0', 0),
    ('pc', 'W0', 0),
    ('ring', 'H2', 1),
    ('ring', 'H1', 1),
    ('side', 'W0', 1),
    ('ring', 'W0', 2),
    ('full', 'W0', 1),
    ('pc', 'W0', 1),
    ('ring', 'H0', 1),
    ('ring', 'W1', 0),
    ('ring', 'H2', 2),
    ('side', 'W0', 2),
    ('ring', 'H1', 2),
    ('full', 'W0', 2),
    ('pc', 'W0', 2),
    ('ring', 'W0', 3),
    ('ring', 'H0', 2),
    ('side', 'W1', 0),
    ('full', 'W1', 0),
    ('pc', 'W1', 0),
    ('ring', 'W1', 1),
    ('send', 'O1'),
    ('ring', 'H2', 3),
    ('side', 'W0', 3),
    ('hn', 2),
    ('ring', 'H1', 3),
    ('full', 'W0', 3),
    ('hn', 1),
    ('pc', 'W0', 3),
    ('ring', 'H0', 3),
    ('send', 'O0'),
    ('hn', 0),
    ('ph', 'W0', None, 'own'),
    ('ph', 'W0', None, 0),
    ('ph', 'W0', None, 1),
    ('ring', 'W1', 2),
    ('ph', 'W0', None, 2),
    ('ring', 'O1', 0),
    ('ph', 'W0', None, 3),
    ('side', 'W1', 1),
    ('full', 'O1', 0),
    ('ring', 'O0', 0),
    ('ph', 'W1', None, 'own'),
    ('full', 'W1', 1),
    ('full', 'O0', 0),
    ('pc', 'W1', 1),
    ('ring', 'W1', 3),
    ('ph', 'W1', None, 0),
    ('ring', 'O1', 1),
    ('ph', 'W1', None, 1),
    ('full', 'O1', 1),
    ('ring', 'O0', 1),
    ('at', 'near', 'W0', None),
    ('full', 'O0', 1),
    ('at', 'far', 'W0', None),
    ('side', 'W1', 2),
    ('ring', 'O1', 2),
    ('full', 'W1', 2),
    ('pc', 'W1', 2),
    ('full', 'O1', 2),
    ('ph', 'W1', None, 2),
    ('ring', 'O0', 2),
    ('side', 'W1', 3),
    ('at', 'near', 'W1', None),
    ('full', 'O0', 2),
    ('ring', 'O1', 3),
    ('full', 'W1', 3),
    ('pc', 'W1', 3),
    ('full', 'O1', 3),
    ('ph', 'W1', None, 3),
    ('ring', 'O0', 3),
    ('at', 'far', 'W1', None),
    ('full', 'O0', 3),
    ('ln',),
    ('out', 0),
    ('out', 1),
    ('out', 2),
    ('out', 3),
)


def fused_kernel(
    length_hbm, tiles_hbm, hist_ref, w_ref, wo_ref, cand_ref, gain_hbm, out_ref,
    length_ref, tiles_ref, gain_ref, cb, hb, wb, ob, nb, hn, pb, kvb, ab, gb,
    ring_send, ring_recv, side_send, side_recv, local_sem,
):
    group = lax.axis_index("group")
    user = lax.axis_index("user")
    me = lax.axis_index("cand")
    place = place_of(me)
    slots = cand_ref.shape[1]
    events = hist_ref.shape[1]

    def shard_at(offset):
        return cand_of((place + offset + RING) % RING)

    core_peer = {"user": 1 - user}
    y_peer = {"group": 1 - group}
    ring_peer = ({"cand": shard_at(1)}, {"cand": shard_at(-1)})
    started = []

    quarter = D // 4
    half = D // 2
    part = half // O_PARTS

    def w_rows(g, u):
        return (2 * g + u) * quarter

    def o_rows(u, k):
        return u * half + k * part

    spans = []
    first = 0
    for size in PIECES:
        spans.append((first * (events // 8), size * (events // 8)))
        first += size

    streams = {}
    for j in range(2):
        streams[("W", j)] = (
            w_ref.at[:, pl.ds(j * quarter, quarter)], wb.at[j], w_rows(group, user), quarter
        )
    for e, (start, size) in enumerate(spans):
        streams[("H", e)] = (hist_ref.at[0], hb, start, size)
    for k in range(O_PARTS):
        streams[("O", k)] = (wo_ref, ob, o_rows(user, k), part)
    names = list(streams)
    sided = [name for name in names if name[0] != "H"]

    def side_rows(name, kind, g, u):
        if name[0] == "W":
            return (w_rows(g, u), w_rows(g, u), w_rows(1 - g, u))[kind], quarter
        return o_rows(u, name[1]), part

    CORE, Y, DIAG = 0, 1, 2

    barrier = pltpu.get_barrier_semaphore()
    for peer in (ring_peer[0], ring_peer[1], core_peer, y_peer):
        pl.semaphore_signal(barrier, inc=1, device_id=peer, device_id_type=MESH)

    fetch = pltpu.make_async_copy(cand_ref.at[0], cb, local_sem.at[4])
    fetch.start()
    own = [
        pltpu.make_async_copy(hist_ref.at[0], hb.at[me], local_sem.at[0]),
        pltpu.make_async_copy(wo_ref, ob.at[me], local_sem.at[1]),
    ]
    for j in range(2):
        own.append(
            pltpu.make_async_copy(streams[("W", j)][0], wb.at[j, me], local_sem.at[2 + j])
        )
    small = [
        pltpu.make_async_copy(length_hbm, length_ref, local_sem.at[5]),
        pltpu.make_async_copy(gain_hbm, gain_ref, local_sem.at[6]),
        pltpu.make_async_copy(tiles_hbm, tiles_ref, local_sem.at[7]),
    ]
    for copy in own + small:
        copy.start()
    pl.semaphore_wait(barrier, 4)

    def ring_copy(name, way, step, shard, first):
        source, buffer, start, size = streams[name]
        if step == 3:
            size = size // 2
            start = start + way * size
        rows = pl.ds(start if isinstance(start, int) else pl.multiple_of(start, 64), size)
        spot = buffer.at[shard, rows, :]
        index = names.index(name)
        return pltpu.make_async_remote_copy(
            src_ref=source.at[rows, :] if first else spot,
            dst_ref=spot,
            send_sem=ring_send.at[index, way, step],
            recv_sem=ring_recv.at[index, way, step],
            device_id=ring_peer[way],
            device_id_type=MESH,
        )

    def ring_start(name, step):
        for way in range(2):
            shard = shard_at(-step if way == 0 else step)
            copy = ring_copy(name, way, step, shard, step == 0)
            copy.start()
            started.append(copy)

    def ring_wait(name, step):
        for way in range(2):
            shard = shard_at(-1 - step if way == 0 else step + 1)
            ring_copy(name, way, step, shard, False).wait_recv()

    def spots(step):
        return ((6, 4),) if step == 3 else ((2 * step, -1 - step), (2 * step + 1, step + 1))

    def side_copy(name, kind, index, offset, g, u):
        start, size = side_rows(name, kind, g, u)
        spot = streams[name][1].at[shard_at(offset), pl.ds(pl.multiple_of(start, 128), size), :]
        place_in = 3 * sided.index(name) + kind
        return pltpu.make_async_remote_copy(
            src_ref=spot, dst_ref=spot,
            send_sem=side_send.at[place_in, index], recv_sem=side_recv.at[place_in, index],
            device_id=y_peer if kind == Y else core_peer, device_id_type=MESH,
        )

    def side_start(name, kind, step):
        for index, offset in spots(step):
            copy = side_copy(name, kind, index, offset, group, user)
            copy.start()
            started.append(copy)

    def side_wait(name, kind, step):
        g, u = (1 - group, user) if kind == Y else (group, 1 - user)
        for index, offset in spots(step):
            side_copy(name, kind, index, offset, g, u).wait_recv()

    def take_ring(name, step):
        ring_wait(name, step)
        if step < 3:
            ring_start(name, step + 1)
        if name[0] == "W":
            side_start(name, Y, step)
        if name in sided:
            side_start(name, CORE, step)

    def take_side(name, step):
        side_wait(name, Y, step)
        side_start(name, DIAG, step)

    def take_core(name, step):
        side_wait(name, CORE, step)
        if name[0] == "W":
            side_wait(name, DIAG, step)

    def over(step, body):
        if step == "own":
            body(me)
        elif step == 3:
            body(shard_at(4))
        else:
            @pl.loop(0, 2)
            def _(way):
                body(shard_at((1 - 2 * way) * (step + 1)))

    def project_cand(j, shard):
        product = jnp.dot(nb[...], wb[j, shard], preferred_element_type=jnp.float32)
        act = half_silu(product).astype(jnp.bfloat16)
        for i in range(2):
            pb[4 * shard + 2 * j + i] = act[:, i * DH : (i + 1) * DH]

    def norm_hist(e):
        length = length_ref[0]
        start, size = spans[e]
        chunk = 128

        @pl.loop(0, size // chunk)
        def _(i):
            first = pl.multiple_of(start + i * chunk, chunk)
            rows = pl.ds(first, chunk)
            whole = jnp.concatenate([hb[c, rows, :] for c in range(RING)], axis=1)
            event = lax.broadcasted_iota(jnp.int32, (chunk, 1), 0) + first
            kept = jnp.where(event < length, 0.5, 0.0)
            hn[rows, :] = layer_norm(whole.astype(jnp.float32), kept).astype(jnp.bfloat16)

    def project_hist(j, e, shard):
        start, size = (0, events) if e is None else spans[e]

        @pl.when((shard % 4) // 2 == 1)
        def _():
            first = 4 * shard - 8 - 8 * (shard // 4) + 2 * j
            rows = pl.ds(start, size)
            product = jnp.dot(hn[rows, :], wb[j, shard], preferred_element_type=jnp.float32)
            act = half_silu(product).astype(jnp.bfloat16)
            for i in range(2):
                kvb[first + i, rows, :] = act[:, i * DH : (i + 1) * DH]

    half_scale = 0.5 / math.sqrt(DH)
    near = (HEADS // 2) * (me % 2)

    def attend(first, e, fresh):
        rows = pl.ds(*((0, events) if e is None else spans[e]))
        for i in range(2):
            head = first + i
            query = pb[2 * HEADS + head]
            scores = lax.dot_general(
                query, kvb[HEADS + head, rows, :], (((1,), (1,)), ((), ())),
                preferred_element_type=jnp.float32,
            )
            weights = half_silu(scores * half_scale).astype(jnp.bfloat16)
            mixed = jnp.dot(weights, kvb[head, rows, :], preferred_element_type=jnp.float32)
            if fresh:
                own_sum = jnp.sum(
                    query.astype(jnp.float32) * pb[3 * HEADS + head].astype(jnp.float32),
                    axis=-1, keepdims=True,
                )
                own_weight = half_silu(own_sum * half_scale)
                ab[head] = mixed + own_weight * pb[HEADS + head].astype(jnp.float32)
            else:
                ab[head] += mixed

    def gate_rows():
        chunk = 128

        @pl.loop(0, slots // chunk)
        def _(i):
            rows = pl.ds(pl.multiple_of(i * chunk, chunk), chunk)
            attn = jnp.concatenate([ab[h, rows, :] for h in range(HEADS)], axis=1)
            gate = jnp.concatenate([pb[h, rows, :] for h in range(HEADS)], axis=1)
            gb[rows, :] = (
                layer_norm(attn) * gain_ref[...] * gate.astype(jnp.float32)
            ).astype(jnp.bfloat16)

    def project_out(step):
        shards = (me, shard_at(4)) if step == 3 else (shard_at(-1 - step), shard_at(step + 1))
        pair = jnp.concatenate([ob[shard] for shard in shards], axis=1)
        added = jnp.dot(gb[...], pair, preferred_element_type=jnp.float32)
        slot = lax.broadcasted_iota(jnp.int32, (slots, 1), 0)
        live = slot < tiles_ref[0, 0] * TILE
        for i, shard in enumerate(shards):
            columns = pl.ds(pl.multiple_of(shard * DH, DH), DH)
            result = cb[:, columns].astype(jnp.float32) + added[:, i * DH : (i + 1) * DH]
            out_ref[0, :, columns] = jnp.where(live, result, 0.0).astype(jnp.bfloat16)

    seen = set()
    for what, *rest in PLAN:
        if what in ("send", "ring", "side", "full"):
            name = (rest[0][0], int(rest[0][1:] or 0))
            if what == "send":
                ring_start(name, 0)
            else:
                {"ring": take_ring, "side": take_side, "full": take_core}[what](name, rest[1])
        elif what == "nb":
            fetch.wait()
            nb[...] = layer_norm(cb[...].astype(jnp.float32), 0.5).astype(jnp.bfloat16)
            for copy in own + small:
                copy.wait()
        elif what == "pc":
            over(rest[1], functools.partial(project_cand, int(rest[0][1])))
        elif what == "hn":
            norm_hist(rest[0])
        elif what == "ph":
            over(rest[2], functools.partial(project_hist, int(rest[0][1]), rest[1]))
        elif what == "at":
            j = int(rest[1][1])
            first = (near if rest[0] == "near" else HEADS // 2 - near) + 2 * j
            attend(first, rest[2], (rest[0], j) not in seen)
            seen.add((rest[0], j))
        elif what == "ln":
            gate_rows()
        else:
            project_out(rest[0])

    for copy in started:
        copy.wait_send()


def fused_shards(history, hist_len, tile_counts, cand_emb, w_in, out_gain, w_out):
    slots = cand_emb.shape[1]
    events = history.shape[1]
    blocks = 4 * D // DH
    anywhere = pl.BlockSpec(memory_space=pl.ANY)
    count = 2 + len(PIECES) + O_PARTS
    return pl.pallas_call(
        fused_kernel,
        out_shape=pltpu.VMEM(cand_emb.shape, jnp.bfloat16),
        in_specs=[anywhere] * 7,
        out_specs=pl.BlockSpec(memory_space=pltpu.VMEM),
        scratch_shapes=[
            pltpu.SMEM((1,), jnp.int32),
            pltpu.SMEM((1, 1), jnp.int32),
            pltpu.VMEM((1, D), jnp.float32),
            pltpu.VMEM((slots, D), jnp.bfloat16),
            pltpu.VMEM((RING, events, D // RING), jnp.bfloat16),
            pltpu.VMEM((2, RING, D, 2 * D // RING), jnp.bfloat16),
            pltpu.VMEM((RING, D, D // RING), jnp.bfloat16),
            pltpu.VMEM((slots, D), jnp.bfloat16),
            pltpu.VMEM((events, D), jnp.bfloat16),
            pltpu.VMEM((blocks, slots, DH), jnp.bfloat16),
            pltpu.VMEM((blocks // 2, events, DH), jnp.bfloat16),
            pltpu.VMEM((HEADS, slots, DH), jnp.float32),
            pltpu.VMEM((slots, D), jnp.bfloat16),
            pltpu.SemaphoreType.DMA((count, 2, 4)),
            pltpu.SemaphoreType.DMA((count, 2, 4)),
            pltpu.SemaphoreType.DMA((6 + 3 * O_PARTS, 7)),
            pltpu.SemaphoreType.DMA((6 + 3 * O_PARTS, 7)),
            pltpu.SemaphoreType.DMA((8,)),
        ],
        compiler_params=pltpu.CompilerParams(
            collective_id=0, has_side_effects=True, vmem_limit_bytes=56 * 1024 * 1024
        ),
        name="score_fused",
    )(hist_len, tile_counts, history, w_in, w_out, cand_emb, out_gain.reshape(1, D))


def attend_rows(carry, kv_piece, queries, length, score_scale):
    key_count = kv_piece.shape[0]
    values = kv_piece[:, :D].reshape(key_count, HEADS, DH)
    key_heads = kv_piece[:, D:].reshape(key_count, HEADS, DH)
    scores = (
        jnp.einsum("rhe,the->hrt", queries, key_heads, preferred_element_type=jnp.float32)
        * score_scale
    )
    positions = jnp.arange(key_count, dtype=jnp.int32)
    weights = jnp.where(positions[None, None, :] < length, jax.nn.silu(scores), 0.0).astype(
        jnp.bfloat16
    )
    mixed_sum = jnp.einsum("hrt,the->rhe", weights, values, preferred_element_type=jnp.float32)
    return mixed_sum.reshape(carry.shape)


def score_rows(embedded, history, length, w_in, out_gain, w_out):
    score_scale = 1.0 / math.sqrt(DH)
    rows_here = embedded.shape[0]
    normed = layer_norm(embedded.astype(jnp.float32)).astype(jnp.bfloat16)
    initial = jnp.zeros((rows_here, D), jnp.float32)
    own_events = lax.all_to_all(history, "cand", split_axis=0, concat_axis=1, tiled=True)
    hist_normed = layer_norm(own_events.astype(jnp.float32)).astype(jnp.bfloat16)
    stacked = jnp.concatenate([normed, hist_normed], axis=0)
    projected = jax.nn.silu(
        jnp.dot(
            stacked,
            lax.all_gather(w_in, "cand", axis=1, tiled=True),
            preferred_element_type=jnp.float32,
        )
    ).astype(jnp.bfloat16)
    proj_rows = projected[:rows_here]
    hist_proj = projected[rows_here:]
    kv_local = jnp.concatenate([hist_proj[:, D : 2 * D], hist_proj[:, 3 * D :]], axis=1)
    queries = proj_rows[:, 2 * D : 3 * D].reshape(rows_here, HEADS, DH)
    summed = attend_rows(
        initial, lax.all_gather(kv_local, "cand", axis=0, tiled=True), queries, length, score_scale
    )
    gate_part = proj_rows[:, :D].astype(jnp.float32)
    cand_values = proj_rows[:, D : 2 * D].reshape(rows_here, HEADS, DH).astype(jnp.float32)
    cand_keys = proj_rows[:, 3 * D :].reshape(rows_here, HEADS, DH).astype(jnp.float32)
    own_score = jax.nn.silu(jnp.sum(queries.astype(jnp.float32) * cand_keys, axis=-1) * score_scale)
    attn = summed + (own_score[:, :, None] * cand_values).reshape(rows_here, D)
    gated = (layer_norm(attn) * out_gain[None, :] * gate_part).astype(jnp.bfloat16)
    residual = embedded.astype(jnp.float32)
    return (
        residual
        + jnp.dot(
            gated,
            lax.all_gather(w_out, "cand", axis=1, tiled=True),
            preferred_element_type=jnp.float32,
        )
    ).astype(jnp.bfloat16)


def shards(history, hist_len, tile_counts, cand_emb, w_in, out_gain, w_out):
    tile_total = tile_counts[0, 0]
    length = hist_len[0]
    slot_rows = cand_emb[0]
    slot_count = slot_rows.shape[0]
    own_history = history[0]
    scored = score_rows(slot_rows, own_history, length, w_in, out_gain, w_out)
    live = jnp.arange(slot_count, dtype=jnp.int32) < tile_total * TILE
    result = jnp.where(live[:, None], scored, jnp.zeros_like(scored))
    return result[None]


def solution(mesh):
    in_specs = (
        P(("group", "user"), None, "cand"),
        P(("group", "user")),
        P(("group", "user"), "cand"),
        P(("group", "user"), "cand", None),
        P(None, "cand"),
        P(),
        P(None, "cand"),
    )
    out_specs = P(("group", "user"), "cand", None)
    sizes = tuple(mesh.shape[name] for name in ("group", "user", "cand"))
    body = fused_shards if sizes == (2, 2, RING) else shards
    return jax.shard_map(body, mesh=mesh, in_specs=in_specs, out_specs=out_specs, check_vma=False)
```

```python
import functools
import math

import jax
import jax.numpy as jnp
from jax import lax
from jax.experimental import pallas as pl
from jax.experimental.pallas import tpu as pltpu
from jax.sharding import PartitionSpec as P

D = 1024
HEADS = 8
DH = 128
TILE = 128
RING = 8
MESH = pl.DeviceIdType.MESH


def layer_norm(values, scale=1.0):
    center = values - jnp.mean(values, axis=-1, keepdims=True)
    spread = jnp.mean(center * center, axis=-1, keepdims=True)
    return center * (lax.rsqrt(spread + 1e-05) * scale)


def half_silu(half):
    return half + half * jnp.tanh(half)


def cand_of(place):
    high = place // 4
    return (1 - high) * (2 * place) + high * (15 - 2 * place)


def place_of(cand):
    row, column = cand // 2, cand % 2
    return (1 - column) * row + column * (7 - row)


PIECES = (5, 3)
O_APART = 64

KV_ORDER = (0o3111, 0o4336, 0o1443, 0o6664)

PLAN = (
    ('send', 'O1', 0),
    ('send', 'W1', 0),
    ('send', 'W0', 0),
    ('send', 'H0', 0),
    ('nb',),
    ('pc', 'W1', 'own'),
    ('pc', 'W0', 'own'),
    ('recv', 'O1', 0),
    ('recv', 'W1', 0),
    ('send', 'W1', 1),
    ('send', 'H1', 0),
    ('side', 'O1', 0),
    ('full', 'O1', 0),
    ('recv', 'W0', 0),
    ('send', 'W0', 1),
    ('send', 'O1', 1),
    ('recv', 'H0', 0),
    ('send', 'H0', 1),
    ('side', 'W1', 0),
    ('recv', 'W1', 1),
    ('full', 'W1', 0),
    ('pc', 'W1', 0),
    ('recv', 'H1', 0),
    ('side', 'W0', 0),
    ('recv', 'W0', 1),
    ('recv', 'O1', 1),
    ('send', 'O1', 2),
    ('send', 'W1', 2),
    ('full', 'W0', 0),
    ('pc', 'W0', 0),
    ('recv', 'H0', 1),
    ('send', 'H0', 2),
    ('send', 'H1', 1),
    ('recv', 'O1', 2),
    ('side', 'W1', 1),
    ('full', 'W1', 1),
    ('pc', 'W1', 1),
    ('recv', 'W1', 2),
    ('send', 'W1', 3),
    ('send', 'O1', 3),
    ('recv', 'H0', 2),
    ('send', 'H0', 3),
    ('send', 'W0', 2),
    ('side', 'W0', 1),
    ('side', 'O1', 1),
    ('full', 'W0', 1),
    ('side', 'O1', 2),
    ('recv', 'H1', 1),
    ('send', 'H1', 2),
    ('send', 'O0', 0),
    ('full', 'O1', 1),
    ('pc', 'W0', 1),
    ('full', 'O1', 2),
    ('recv', 'W1', 3),
    ('recv', 'O1', 3),
    ('recv', 'H0', 3),
    ('hn', 0),
    ('ph', 'W1', 0, 0),
    ('ph', 'W1', 0, 1),
    ('side', 'W1', 2),
    ('ph', 'W0', 0, 1),
    ('ph', 'W0', 0, 0),
    ('recv', 'W0', 2),
    ('send', 'W0', 3),
    ('full', 'W1', 2),
    ('ph', 'W1', 0, 2),
    ('pc', 'W1', 2),
    ('side', 'W1', 3),
    ('recv', 'H1', 2),
    ('send', 'H1', 3),
    ('side', 'O1', 3),
    ('at', 'near', 'W1', 0),
    ('full', 'W1', 3),
    ('pc', 'W1', 3),
    ('full', 'O1', 3),
    ('ph', 'W1', 0, 3),
    ('recv', 'O0', 0),
    ('send', 'O0', 1),
    ('at', 'far', 'W1', 0),
    ('recv', 'W0', 3),
    ('full', 'O0', 0),
    ('recv', 'H1', 3),
    ('hn', 1),
    ('ph', 'W1', 1, 2),
    ('ph', 'W1', 1, 3),
    ('ph', 'W1', 1, 1),
    ('ph', 'W0', 1, 1),
    ('side', 'W0', 2),
    ('ph', 'W0', 1, 0),
    ('ph', 'W1', 1, 0),
    ('recv', 'O0', 1),
    ('send', 'O0', 2),
    ('at', 'near', 'W1', 1),
    ('full', 'W0', 2),
    ('ph', 'W0', 0, 2),
    ('full', 'O0', 1),
    ('ph', 'W0', 1, 2),
    ('side', 'W0', 3),
    ('at', 'far', 'W1', 1),
    ('pc', 'W0', 2),
    ('at', 'near', 'W0', 0),
    ('full', 'W0', 3),
    ('pc', 'W0', 3),
    ('recv', 'O0', 2),
    ('send', 'O0', 3),
    ('ph', 'W0', 1, 3),
    ('ph', 'W0', 0, 3),
    ('at', 'far', 'W0', 0),
    ('full', 'O0', 2),
    ('at', 'near', 'W0', 1),
    ('at', 'far', 'W0', 1),
    ('ln',),
    ('recv', 'O0', 3),
    ('out', 1),
    ('out', 2),
    ('out', 0),
    ('full', 'O0', 3),
    ('out', 3),
)


def fused_kernel(
    length_hbm, tiles_hbm, hist_ref, w_ref, wo_ref, cand_ref, gain_hbm, out_ref,
    length_ref, tiles_ref, gain_ref, cb, hb, wb, ob, nb, hn, pb, kvb, ab, gb,
    ring_send, ring_recv, side_send, side_recv, local_sem,
):
    group = lax.axis_index("group")
    user = lax.axis_index("user")
    me = lax.axis_index("cand")
    place = place_of(me)
    slots = cand_ref.shape[1]
    events = hist_ref.shape[1]

    def shard_at(offset):
        return cand_of((place + offset + RING) % RING)

    core_peer = {"user": 1 - user}
    y_peer = {"group": 1 - group}
    ring_peer = ({"cand": shard_at(1)}, {"cand": shard_at(-1)})
    started = []

    quarter = D // 4
    half = D // 2

    def w_rows(g, u):
        return (2 * g + u) * quarter

    def o_rows(g, u):
        return u * half + g * (half - O_APART)

    spans = []
    first = 0
    for size in PIECES:
        spans.append((first * (events // 8), size * (events // 8)))
        first += size

    streams = {}
    for j in range(2):
        streams[("W", j)] = (
            w_ref.at[:, pl.ds(j * quarter, quarter)], wb.at[j], w_rows(group, user), quarter
        )
    for e, (start, size) in enumerate(spans):
        streams[("H", e)] = (hist_ref.at[0], hb, start, size)
    streams[("O", 0)] = (wo_ref, ob, user * half + O_APART, half - 2 * O_APART)
    if O_APART:
        streams[("O", 1)] = (wo_ref, ob, o_rows(group, user), O_APART)
    names = list(streams)
    sided = [name for name in names if name[0] != "H"]
    shared = [name for name in sided if name != ("O", 0)]

    def side_rows(name, kind, g, u):
        if name[0] == "W":
            return (w_rows(g, u), w_rows(g, u), w_rows(1 - g, u))[kind], quarter
        if name[1] == 0:
            return u * half + O_APART, half - 2 * O_APART
        return (o_rows(g, u), o_rows(g, u), o_rows(1 - g, u))[kind], O_APART

    CORE, Y, DIAG = 0, 1, 2

    barrier = pltpu.get_barrier_semaphore()
    for peer in (ring_peer[0], ring_peer[1], core_peer, y_peer):
        pl.semaphore_signal(barrier, inc=1, device_id=peer, device_id_type=MESH)

    fetch = pltpu.make_async_copy(cand_ref.at[0], cb, local_sem.at[4])
    fetch.start()
    own = [
        pltpu.make_async_copy(hist_ref.at[0], hb.at[me], local_sem.at[0]),
        pltpu.make_async_copy(wo_ref, ob.at[me], local_sem.at[1]),
    ]
    for j in range(2):
        own.append(
            pltpu.make_async_copy(streams[("W", j)][0], wb.at[j, me], local_sem.at[2 + j])
        )
    small = [
        pltpu.make_async_copy(length_hbm, length_ref, local_sem.at[5]),
        pltpu.make_async_copy(gain_hbm, gain_ref, local_sem.at[6]),
        pltpu.make_async_copy(tiles_hbm, tiles_ref, local_sem.at[7]),
    ]
    for copy in own + small:
        copy.start()
    pl.semaphore_wait(barrier, 4)

    def ring_copy(name, way, step, shard, first):
        source, buffer, start, size = streams[name]
        if step == 3:
            size = size // 2
            start = start + way * size
        rows = pl.ds(start if isinstance(start, int) else pl.multiple_of(start, 16), size)
        spot = buffer.at[shard, rows, :]
        index = names.index(name)
        return pltpu.make_async_remote_copy(
            src_ref=source.at[rows, :] if first else spot,
            dst_ref=spot,
            send_sem=ring_send.at[index, way, step],
            recv_sem=ring_recv.at[index, way, step],
            device_id=ring_peer[way],
            device_id_type=MESH,
        )

    def ring_start(name, step):
        for way in range(2):
            shard = shard_at(-step if way == 0 else step)
            copy = ring_copy(name, way, step, shard, step == 0)
            copy.start()
            started.append(copy)

    def ring_wait(name, step):
        for way in range(2):
            shard = shard_at(-1 - step if way == 0 else step + 1)
            ring_copy(name, way, step, shard, False).wait_recv()

    def spots(step):
        return ((6, 4),) if step == 3 else ((2 * step, -1 - step), (2 * step + 1, step + 1))

    def side_copy(name, kind, index, offset, g, u):
        start, size = side_rows(name, kind, g, u)
        spot = streams[name][1].at[shard_at(offset), pl.ds(pl.multiple_of(start, 16), size), :]
        place_in = 3 * sided.index(name) + kind
        return pltpu.make_async_remote_copy(
            src_ref=spot, dst_ref=spot,
            send_sem=side_send.at[place_in, index], recv_sem=side_recv.at[place_in, index],
            device_id=y_peer if kind == Y else core_peer, device_id_type=MESH,
        )

    def side_start(name, kind, step):
        for index, offset in spots(step):
            copy = side_copy(name, kind, index, offset, group, user)
            copy.start()
            started.append(copy)

    def side_wait(name, kind, step):
        g, u = (1 - group, user) if kind == Y else (group, 1 - user)
        for index, offset in spots(step):
            side_copy(name, kind, index, offset, g, u).wait_recv()

    def take_ring(name, step):
        ring_wait(name, step)
        if name in shared:
            side_start(name, Y, step)
        if name in sided:
            side_start(name, CORE, step)

    def take_side(name, step):
        side_wait(name, Y, step)
        side_start(name, DIAG, step)

    def take_core(name, step):
        side_wait(name, CORE, step)
        if name in shared:
            side_wait(name, DIAG, step)

    def over(step, body):
        if step == "own":
            body(me)
        elif step == 3:
            body(shard_at(4))
        else:
            for way in range(2):
                body(shard_at((1 - 2 * way) * (step + 1)))

    def project_cand(j, shard):
        product = jnp.dot(nb[...], wb[j, shard], preferred_element_type=jnp.float32)
        act = half_silu(product).astype(jnp.bfloat16)
        for i in range(2):
            pb[4 * shard + 2 * j + i] = act[:, i * DH : (i + 1) * DH]

    def norm_hist(e):
        length = length_ref[0]
        start, size = spans[e]
        chunk = 128

        @pl.loop(0, size // chunk)
        def _(i):
            first = pl.multiple_of(start + i * chunk, chunk)
            rows = pl.ds(first, chunk)
            whole = jnp.concatenate([hb[c, rows, :] for c in range(RING)], axis=1)
            event = lax.broadcasted_iota(jnp.int32, (chunk, 1), 0) + first
            kept = jnp.where(event < length, 0.5, 0.0)
            hn[rows, :] = layer_norm(whole.astype(jnp.float32), kept).astype(jnp.bfloat16)

    high = place // 4
    low = (1 - high) * place + high * (RING - 1 - place)
    digit = (1 + 7 * (low % 2)) * (1 + 63 * (low // 2))

    def project_hist(j, e, turn):
        start, size = (0, events) if e is None else spans[e]
        owner = (KV_ORDER[turn] // digit) % 8
        shard = cand_of((1 - high) * owner + high * (RING - 1 - owner))
        first = 4 * shard - 8 - 8 * (shard // 4) + 2 * j
        rows = pl.ds(start, size)
        product = jnp.dot(hn[rows, :], wb[j, shard], preferred_element_type=jnp.float32)
        act = half_silu(product).astype(jnp.bfloat16)
        for i in range(2):
            kvb[first + i, rows, :] = act[:, i * DH : (i + 1) * DH]

    half_scale = 0.5 / math.sqrt(DH)
    near = (HEADS // 2) * (me % 2)

    def attend(first, e, fresh):
        rows = pl.ds(*((0, events) if e is None else spans[e]))
        for i in range(2):
            head = first + i
            query = pb[2 * HEADS + head]
            scores = lax.dot_general(
                query, kvb[HEADS + head, rows, :], (((1,), (1,)), ((), ())),
                preferred_element_type=jnp.float32,
            )
            weights = half_silu(scores * half_scale).astype(jnp.bfloat16)
            mixed = jnp.dot(weights, kvb[head, rows, :], preferred_element_type=jnp.float32)
            if fresh:
                own_sum = jnp.sum(
                    query.astype(jnp.float32) * pb[3 * HEADS + head].astype(jnp.float32),
                    axis=-1, keepdims=True,
                )
                own_weight = half_silu(own_sum * half_scale)
                ab[head] = mixed + own_weight * pb[HEADS + head].astype(jnp.float32)
            else:
                ab[head] += mixed

    def gate_rows():
        chunk = 128

        @pl.loop(0, slots // chunk)
        def _(i):
            rows = pl.ds(pl.multiple_of(i * chunk, chunk), chunk)
            attn = jnp.concatenate([ab[h, rows, :] for h in range(HEADS)], axis=1)
            gate = jnp.concatenate([pb[h, rows, :] for h in range(HEADS)], axis=1)
            gb[rows, :] = (
                layer_norm(attn) * gain_ref[...] * gate.astype(jnp.float32)
            ).astype(jnp.bfloat16)

    def project_out(step):
        shards = (me, shard_at(4)) if step == 3 else (shard_at(-1 - step), shard_at(step + 1))
        pair = jnp.concatenate([ob[shard] for shard in shards], axis=1)
        added = jnp.dot(gb[...], pair, preferred_element_type=jnp.float32)
        slot = lax.broadcasted_iota(jnp.int32, (slots, 1), 0)
        live = slot < tiles_ref[0, 0] * TILE
        for i, shard in enumerate(shards):
            columns = pl.ds(pl.multiple_of(shard * DH, DH), DH)
            result = cb[:, columns].astype(jnp.float32) + added[:, i * DH : (i + 1) * DH]
            out_ref[0, :, columns] = jnp.where(live, result, 0.0).astype(jnp.bfloat16)

    seen = set()
    for what, *rest in PLAN:
        if what in ("send", "recv", "side", "full"):
            act = {"send": ring_start, "recv": take_ring, "side": take_side, "full": take_core}
            act[what]((rest[0][0], int(rest[0][1])), rest[1])
        elif what == "nb":
            fetch.wait()
            nb[...] = layer_norm(cb[...].astype(jnp.float32), 0.5).astype(jnp.bfloat16)
            for copy in own + small:
                copy.wait()
        elif what == "pc":
            over(rest[1], functools.partial(project_cand, int(rest[0][1])))
        elif what == "hn":
            norm_hist(rest[0])
        elif what == "ph":
            project_hist(int(rest[0][1]), rest[1], rest[2])
        elif what == "at":
            j = int(rest[1][1])
            first = (near if rest[0] == "near" else HEADS // 2 - near) + 2 * j
            attend(first, rest[2], (rest[0], j) not in seen)
            seen.add((rest[0], j))
        elif what == "ln":
            gate_rows()
        else:
            project_out(rest[0])

    for copy in started:
        copy.wait_send()


def fused_shards(history, hist_len, tile_counts, cand_emb, w_in, out_gain, w_out):
    slots = cand_emb.shape[1]
    events = history.shape[1]
    blocks = 4 * D // DH
    anywhere = pl.BlockSpec(memory_space=pl.ANY)
    count = 2 + len(PIECES) + (2 if O_APART else 1)
    return pl.pallas_call(
        fused_kernel,
        out_shape=pltpu.VMEM(cand_emb.shape, jnp.bfloat16),
        in_specs=[anywhere] * 7,
        out_specs=pl.BlockSpec(memory_space=pltpu.VMEM),
        scratch_shapes=[
            pltpu.SMEM((1,), jnp.int32),
            pltpu.SMEM((1, 1), jnp.int32),
            pltpu.VMEM((1, D), jnp.float32),
            pltpu.VMEM((slots, D), jnp.bfloat16),
            pltpu.VMEM((RING, events, D // RING), jnp.bfloat16),
            pltpu.VMEM((2, RING, D, 2 * D // RING), jnp.bfloat16),
            pltpu.VMEM((RING, D, D // RING), jnp.bfloat16),
            pltpu.VMEM((slots, D), jnp.bfloat16),
            pltpu.VMEM((events, D), jnp.bfloat16),
            pltpu.VMEM((blocks, slots, DH), jnp.bfloat16),
            pltpu.VMEM((blocks // 2, events, DH), jnp.bfloat16),
            pltpu.VMEM((HEADS, slots, DH), jnp.float32),
            pltpu.VMEM((slots, D), jnp.bfloat16),
            pltpu.SemaphoreType.DMA((count, 2, 4)),
            pltpu.SemaphoreType.DMA((count, 2, 4)),
            pltpu.SemaphoreType.DMA((12, 7)),
            pltpu.SemaphoreType.DMA((12, 7)),
            pltpu.SemaphoreType.DMA((8,)),
        ],
        compiler_params=pltpu.CompilerParams(
            collective_id=0, has_side_effects=True, vmem_limit_bytes=56 * 1024 * 1024
        ),
        name="score_fused",
    )(hist_len, tile_counts, history, w_in, w_out, cand_emb, out_gain.reshape(1, D))


def attend_rows(carry, kv_piece, queries, length, score_scale):
    key_count = kv_piece.shape[0]
    values = kv_piece[:, :D].reshape(key_count, HEADS, DH)
    key_heads = kv_piece[:, D:].reshape(key_count, HEADS, DH)
    scores = (
        jnp.einsum("rhe,the->hrt", queries, key_heads, preferred_element_type=jnp.float32)
        * score_scale
    )
    positions = jnp.arange(key_count, dtype=jnp.int32)
    weights = jnp.where(positions[None, None, :] < length, jax.nn.silu(scores), 0.0).astype(
        jnp.bfloat16
    )
    mixed_sum = jnp.einsum("hrt,the->rhe", weights, values, preferred_element_type=jnp.float32)
    return mixed_sum.reshape(carry.shape)


def score_rows(embedded, history, length, w_in, out_gain, w_out):
    score_scale = 1.0 / math.sqrt(DH)
    rows_here = embedded.shape[0]
    normed = layer_norm(embedded.astype(jnp.float32)).astype(jnp.bfloat16)
    initial = jnp.zeros((rows_here, D), jnp.float32)
    own_events = lax.all_to_all(history, "cand", split_axis=0, concat_axis=1, tiled=True)
    hist_normed = layer_norm(own_events.astype(jnp.float32)).astype(jnp.bfloat16)
    stacked = jnp.concatenate([normed, hist_normed], axis=0)
    projected = jax.nn.silu(
        jnp.dot(
            stacked,
            lax.all_gather(w_in, "cand", axis=1, tiled=True),
            preferred_element_type=jnp.float32,
        )
    ).astype(jnp.bfloat16)
    proj_rows = projected[:rows_here]
    hist_proj = projected[rows_here:]
    kv_local = jnp.concatenate([hist_proj[:, D : 2 * D], hist_proj[:, 3 * D :]], axis=1)
    queries = proj_rows[:, 2 * D : 3 * D].reshape(rows_here, HEADS, DH)
    summed = attend_rows(
        initial, lax.all_gather(kv_local, "cand", axis=0, tiled=True), queries, length, score_scale
    )
    gate_part = proj_rows[:, :D].astype(jnp.float32)
    cand_values = proj_rows[:, D : 2 * D].reshape(rows_here, HEADS, DH).astype(jnp.float32)
    cand_keys = proj_rows[:, 3 * D :].reshape(rows_here, HEADS, DH).astype(jnp.float32)
    own_score = jax.nn.silu(jnp.sum(queries.astype(jnp.float32) * cand_keys, axis=-1) * score_scale)
    attn = summed + (own_score[:, :, None] * cand_values).reshape(rows_here, D)
    gated = (layer_norm(attn) * out_gain[None, :] * gate_part).astype(jnp.bfloat16)
    residual = embedded.astype(jnp.float32)
    return (
        residual
        + jnp.dot(
            gated,
            lax.all_gather(w_out, "cand", axis=1, tiled=True),
            preferred_element_type=jnp.float32,
        )
    ).astype(jnp.bfloat16)


def shards(history, hist_len, tile_counts, cand_emb, w_in, out_gain, w_out):
    tile_total = tile_counts[0, 0]
    length = hist_len[0]
    slot_rows = cand_emb[0]
    slot_count = slot_rows.shape[0]
    own_history = history[0]
    scored = score_rows(slot_rows, own_history, length, w_in, out_gain, w_out)
    live = jnp.arange(slot_count, dtype=jnp.int32) < tile_total * TILE
    result = jnp.where(live[:, None], scored, jnp.zeros_like(scored))
    return result[None]


def solution(mesh):
    in_specs = (
        P(("group", "user"), None, "cand"),
        P(("group", "user")),
        P(("group", "user"), "cand"),
        P(("group", "user"), "cand", None),
        P(None, "cand"),
        P(),
        P(None, "cand"),
    )
    out_specs = P(("group", "user"), "cand", None)
    sizes = tuple(mesh.shape[name] for name in ("group", "user", "cand"))
    body = fused_shards if sizes == (2, 2, RING) else shards
    return jax.shard_map(body, mesh=mesh, in_specs=in_specs, out_specs=out_specs, check_vma=False)
```

```python
import functools
import math

import jax
import jax.numpy as jnp
from jax import lax
from jax.experimental import pallas as pl
from jax.experimental.pallas import tpu as pltpu
from jax.sharding import PartitionSpec as P

D = 1024
HEADS = 8
DH = 128
TILE = 128
RING = 8
MESH = pl.DeviceIdType.MESH


def layer_norm(values, scale=1.0):
    center = values - jnp.mean(values, axis=-1, keepdims=True)
    spread = jnp.mean(center * center, axis=-1, keepdims=True)
    return center * (lax.rsqrt(spread + 1e-05) * scale)


def half_silu(half):
    return half + half * jnp.tanh(half)


def cand_of(place):
    high = place // 4
    return (1 - high) * (2 * place) + high * (15 - 2 * place)


def place_of(cand):
    row, column = cand // 2, cand % 2
    return (1 - column) * row + column * (7 - row)


PIECES = (5, 3)
O_APART = 64

KV_ORDER = (0o3111, 0o4336, 0o1443, 0o6664)

PLAN = (
    ('send', 'W1', 0),
    ('send', 'W0', 0),
    ('send', 'O1', 0),
    ('send', 'H0', 0),
    ('nb',),
    ('pc', 'W0', 'own'),
    ('pc', 'W1', 'own'),
    ('recv', 'W1', 0),
    ('send', 'W1', 1),
    ('recv', 'W0', 0),
    ('recv', 'O1', 0),
    ('recv', 'H0', 0),
    ('send', 'H0', 1),
    ('side', 'W1', 0),
    ('full', 'W1', 0),
    ('recv', 'W1', 1),
    ('send', 'W1', 2),
    ('send', 'O1', 1),
    ('pc', 'W1', 0),
    ('recv', 'H0', 1),
    ('send', 'H0', 2),
    ('side', 'W0', 0),
    ('side', 'O1', 0),
    ('full', 'W0', 0),
    ('pc', 'W0', 0),
    ('full', 'O1', 0),
    ('recv', 'W1', 2),
    ('send', 'W1', 3),
    ('send', 'H1', 0),
    ('send', 'W0', 1),
    ('recv', 'O1', 1),
    ('send', 'O1', 2),
    ('recv', 'H0', 2),
    ('send', 'H0', 3),
    ('side', 'W1', 1),
    ('recv', 'W1', 3),
    ('full', 'W1', 1),
    ('pc', 'W1', 1),
    ('recv', 'H1', 0),
    ('send', 'H1', 1),
    ('side', 'W1', 2),
    ('recv', 'W0', 1),
    ('send', 'W0', 2),
    ('side', 'O1', 1),
    ('recv', 'O1', 2),
    ('full', 'W1', 2),
    ('pc', 'W1', 2),
    ('full', 'O1', 1),
    ('recv', 'H0', 3),
    ('hn', 0),
    ('side', 'W1', 3),
    ('ph', 'W0', 0, 0),
    ('ph', 'W1', 0, 0),
    ('recv', 'H1', 1),
    ('send', 'H1', 2),
    ('send', 'O0', 0),
    ('send', 'O1', 3),
    ('full', 'W1', 3),
    ('ph', 'W1', 0, 2),
    ('ph', 'W1', 0, 1),
    ('at', 'near', 'W1', 0),
    ('ph', 'W1', 0, 3),
    ('recv', 'W0', 2),
    ('pc', 'W1', 3),
    ('at', 'far', 'W1', 0),
    ('side', 'W0', 1),
    ('recv', 'H1', 2),
    ('send', 'H1', 3),
    ('send', 'W0', 3),
    ('side', 'O1', 2),
    ('full', 'W0', 1),
    ('ph', 'W0', 0, 1),
    ('pc', 'W0', 1),
    ('full', 'O1', 2),
    ('recv', 'O0', 0),
    ('send', 'O0', 1),
    ('recv', 'O1', 3),
    ('recv', 'H1', 3),
    ('hn', 1),
    ('full', 'O0', 0),
    ('ph', 'W0', 1, 1),
    ('ph', 'W1', 1, 3),
    ('recv', 'W0', 3),
    ('ph', 'W1', 1, 0),
    ('ph', 'W1', 1, 2),
    ('ph', 'W1', 1, 1),
    ('side', 'W0', 2),
    ('side', 'O1', 3),
    ('at', 'far', 'W1', 1),
    ('recv', 'O0', 1),
    ('send', 'O0', 2),
    ('at', 'near', 'W1', 1),
    ('full', 'W0', 2),
    ('full', 'O1', 3),
    ('pc', 'W0', 2),
    ('full', 'O0', 1),
    ('ph', 'W0', 1, 2),
    ('ph', 'W0', 0, 2),
    ('at', 'near', 'W0', 0),
    ('side', 'W0', 3),
    ('ph', 'W0', 1, 0),
    ('at', 'near', 'W0', 1),
    ('recv', 'O0', 2),
    ('send', 'O0', 3),
    ('full', 'W0', 3),
    ('pc', 'W0', 3),
    ('ph', 'W0', 0, 3),
    ('at', 'far', 'W0', 0),
    ('full', 'O0', 2),
    ('ph', 'W0', 1, 3),
    ('at', 'far', 'W0', 1),
    ('ln',),
    ('recv', 'O0', 3),
    ('out', 1),
    ('out', 2),
    ('out', 0),
    ('full', 'O0', 3),
    ('out', 3),
)


def fused_kernel(
    length_hbm, tiles_hbm, hist_ref, w_ref, wo_ref, cand_ref, gain_hbm, out_ref,
    length_ref, tiles_ref, gain_ref, cb, hb, wb, ob, nb, hn, pb, kvb, ab, gb,
    ring_send, ring_recv, side_send, side_recv, core_recv, local_sem,
):
    group = lax.axis_index("group")
    user = lax.axis_index("user")
    me = lax.axis_index("cand")
    place = place_of(me)
    slots = cand_ref.shape[1]
    events = hist_ref.shape[1]

    def shard_at(offset):
        return cand_of((place + offset + RING) % RING)

    core_peer = {"user": 1 - user}
    y_peer = {"group": 1 - group}
    ring_peer = ({"cand": shard_at(1)}, {"cand": shard_at(-1)})

    quarter = D // 4
    half = D // 2

    def w_rows(g, u):
        return (2 * g + u) * quarter

    def o_rows(g, u):
        return u * half + g * (half - O_APART)

    spans = []
    first = 0
    for size in PIECES:
        spans.append((first * (events // 8), size * (events // 8)))
        first += size

    streams = {}
    for j in range(2):
        streams[("W", j)] = (
            w_ref.at[:, pl.ds(j * quarter, quarter)], wb.at[j], w_rows(group, user), quarter
        )
    for e, (start, size) in enumerate(spans):
        streams[("H", e)] = (hist_ref.at[0], hb, start, size)
    streams[("O", 0)] = (wo_ref, ob, user * half + O_APART, half - 2 * O_APART)
    if O_APART:
        streams[("O", 1)] = (wo_ref, ob, o_rows(group, user), O_APART)
    names = list(streams)
    sided = [name for name in names if name[0] != "H"]
    shared = [name for name in sided if name != ("O", 0)]

    def side_rows(name, kind, g, u):
        if name[0] == "W":
            return (w_rows(g, u), w_rows(g, u), w_rows(1 - g, u))[kind], quarter
        if name[1] == 0:
            return u * half + O_APART, half - 2 * O_APART
        return (o_rows(g, u), o_rows(g, u), o_rows(1 - g, u))[kind], O_APART

    CORE, Y, DIAG = 0, 1, 2

    barrier = pltpu.get_barrier_semaphore()
    for peer in (ring_peer[0], ring_peer[1], core_peer, y_peer):
        pl.semaphore_signal(barrier, inc=1, device_id=peer, device_id_type=MESH)

    fetch = pltpu.make_async_copy(cand_ref.at[0], cb, local_sem.at[4])
    fetch.start()
    own = [
        pltpu.make_async_copy(hist_ref.at[0], hb.at[me], local_sem.at[0]),
        pltpu.make_async_copy(wo_ref, ob.at[me], local_sem.at[1]),
    ]
    for j in range(2):
        own.append(
            pltpu.make_async_copy(streams[("W", j)][0], wb.at[j, me], local_sem.at[2 + j])
        )
    small = [
        pltpu.make_async_copy(length_hbm, length_ref, local_sem.at[5]),
        pltpu.make_async_copy(gain_hbm, gain_ref, local_sem.at[6]),
        pltpu.make_async_copy(tiles_hbm, tiles_ref, local_sem.at[7]),
    ]
    for copy in own + small:
        copy.start()
    pl.semaphore_wait(barrier, 4)

    def ring_copy(name, way, step, shard, first):
        source, buffer, start, size = streams[name]
        if step == 3:
            size = size // 2
            start = start + way * size
        rows = pl.ds(start if isinstance(start, int) else pl.multiple_of(start, 16), size)
        spot = buffer.at[shard, rows, :]
        index = names.index(name)
        return pltpu.make_async_remote_copy(
            src_ref=source.at[rows, :] if first else spot,
            dst_ref=spot,
            send_sem=ring_send.at[index],
            recv_sem=ring_recv.at[index, step],
            device_id=ring_peer[way],
            device_id_type=MESH,
        )

    def landed(name, shards, rows):
        return streams[name][1].at[pl.ds(0, shards), pl.ds(0, rows), :]

    def wait_for(sem, spot):
        pltpu.make_async_copy(spot, spot, sem).wait()

    def ring_start(name, step):
        for way in range(2):
            shard = shard_at(-step if way == 0 else step)
            ring_copy(name, way, step, shard, step == 0).start()

    def ring_wait(name, step):
        size = streams[name][3]
        shards = 1 if step == 3 else 2
        wait_for(ring_recv.at[names.index(name), step], landed(name, shards, size))

    def spots(step):
        return (4,) if step == 3 else (-1 - step, step + 1)

    def side_start(name, kind, step):
        start, size = side_rows(name, kind, group, user)
        index = sided.index(name)
        for offset in spots(step):
            spot = streams[name][1].at[
                shard_at(offset), pl.ds(pl.multiple_of(start, 16), size), :
            ]
            pltpu.make_async_remote_copy(
                src_ref=spot, dst_ref=spot,
                send_sem=side_send.at[3 * index + kind],
                recv_sem=(side_recv if kind == Y else core_recv).at[index, step],
                device_id=y_peer if kind == Y else core_peer, device_id_type=MESH,
            ).start()

    def take_ring(name, step):
        ring_wait(name, step)
        if name in shared:
            side_start(name, Y, step)
        if name in sided:
            side_start(name, CORE, step)

    def take_side(name, step):
        rows = side_rows(name, Y, group, user)[1]
        wait_for(side_recv.at[sided.index(name), step], landed(name, len(spots(step)), rows))
        side_start(name, DIAG, step)

    def take_core(name, step):
        rows = side_rows(name, CORE, group, user)[1]
        if name in shared:
            rows = 2 * rows
        wait_for(core_recv.at[sided.index(name), step], landed(name, len(spots(step)), rows))

    def over(step, body):
        if step == "own":
            body(me)
        elif step == 3:
            body(shard_at(4))
        else:
            for way in range(2):
                body(shard_at((1 - 2 * way) * (step + 1)))

    def project_cand(j, shard):
        product = jnp.dot(nb[...], wb[j, shard], preferred_element_type=jnp.float32)
        act = half_silu(product).astype(jnp.bfloat16)
        for i in range(2):
            pb[4 * shard + 2 * j + i] = act[:, i * DH : (i + 1) * DH]

    def norm_hist(e):
        length = length_ref[0]
        start, size = spans[e]
        chunk = 128

        @pl.loop(0, size // chunk)
        def _(i):
            first = pl.multiple_of(start + i * chunk, chunk)
            rows = pl.ds(first, chunk)
            whole = jnp.concatenate([hb[c, rows, :] for c in range(RING)], axis=1)
            event = lax.broadcasted_iota(jnp.int32, (chunk, 1), 0) + first
            kept = jnp.where(event < length, 0.5, 0.0)
            hn[rows, :] = layer_norm(whole.astype(jnp.float32), kept).astype(jnp.bfloat16)

    high = place // 4
    low = (1 - high) * place + high * (RING - 1 - place)
    digit = (1 + 7 * (low % 2)) * (1 + 63 * (low // 2))

    def project_hist(j, e, turn):
        start, size = (0, events) if e is None else spans[e]
        owner = (KV_ORDER[turn] // digit) % 8
        shard = cand_of((1 - high) * owner + high * (RING - 1 - owner))
        first = 4 * shard - 8 - 8 * (shard // 4) + 2 * j
        rows = pl.ds(start, size)
        product = jnp.dot(hn[rows, :], wb[j, shard], preferred_element_type=jnp.float32)
        act = half_silu(product).astype(jnp.bfloat16)
        for i in range(2):
            kvb[first + i, rows, :] = act[:, i * DH : (i + 1) * DH]

    half_scale = 0.5 / math.sqrt(DH)
    near = (HEADS // 2) * (me % 2)

    def attend(first, e, fresh):
        rows = pl.ds(*((0, events) if e is None else spans[e]))
        for i in range(2):
            head = first + i
            query = pb[2 * HEADS + head]
            scores = lax.dot_general(
                query, kvb[HEADS + head, rows, :], (((1,), (1,)), ((), ())),
                preferred_element_type=jnp.float32,
            )
            weights = half_silu(scores * half_scale).astype(jnp.bfloat16)
            mixed = jnp.dot(weights, kvb[head, rows, :], preferred_element_type=jnp.float32)
            if fresh:
                own_sum = jnp.sum(
                    query.astype(jnp.float32) * pb[3 * HEADS + head].astype(jnp.float32),
                    axis=-1, keepdims=True,
                )
                own_weight = half_silu(own_sum * half_scale)
                ab[head] = mixed + own_weight * pb[HEADS + head].astype(jnp.float32)
            else:
                ab[head] += mixed

    def gate_rows():
        chunk = 128

        @pl.loop(0, slots // chunk)
        def _(i):
            rows = pl.ds(pl.multiple_of(i * chunk, chunk), chunk)
            attn = jnp.concatenate([ab[h, rows, :] for h in range(HEADS)], axis=1)
            gate = jnp.concatenate([pb[h, rows, :] for h in range(HEADS)], axis=1)
            gb[rows, :] = (
                layer_norm(attn) * gain_ref[...] * gate.astype(jnp.float32)
            ).astype(jnp.bfloat16)

    def project_out(step):
        shards = (me, shard_at(4)) if step == 3 else (shard_at(-1 - step), shard_at(step + 1))
        pair = jnp.concatenate([ob[shard] for shard in shards], axis=1)
        added = jnp.dot(gb[...], pair, preferred_element_type=jnp.float32)
        slot = lax.broadcasted_iota(jnp.int32, (slots, 1), 0)
        live = slot < tiles_ref[0, 0] * TILE
        for i, shard in enumerate(shards):
            columns = pl.ds(pl.multiple_of(shard * DH, DH), DH)
            result = cb[:, columns].astype(jnp.float32) + added[:, i * DH : (i + 1) * DH]
            out_ref[0, :, columns] = jnp.where(live, result, 0.0).astype(jnp.bfloat16)

    seen = set()
    for what, *rest in PLAN:
        if what in ("send", "recv", "side", "full"):
            act = {"send": ring_start, "recv": take_ring, "side": take_side, "full": take_core}
            act[what]((rest[0][0], int(rest[0][1])), rest[1])
        elif what == "nb":
            fetch.wait()
            nb[...] = layer_norm(cb[...].astype(jnp.float32), 0.5).astype(jnp.bfloat16)
            for copy in own + small:
                copy.wait()
        elif what == "pc":
            over(rest[1], functools.partial(project_cand, int(rest[0][1])))
        elif what == "hn":
            norm_hist(rest[0])
        elif what == "ph":
            project_hist(int(rest[0][1]), rest[1], rest[2])
        elif what == "at":
            j = int(rest[1][1])
            first = (near if rest[0] == "near" else HEADS // 2 - near) + 2 * j
            attend(first, rest[2], (rest[0], j) not in seen)
            seen.add((rest[0], j))
        elif what == "ln":
            gate_rows()
        else:
            project_out(rest[0])

    for name in names:
        wait_for(ring_send.at[names.index(name)], landed(name, RING - 1, streams[name][3]))
    for name in sided:
        for kind in (CORE, Y, DIAG) if name in shared else (CORE,):
            rows = side_rows(name, kind, group, user)[1]
            wait_for(side_send.at[3 * sided.index(name) + kind], landed(name, RING - 1, rows))


def fused_shards(history, hist_len, tile_counts, cand_emb, w_in, out_gain, w_out):
    slots = cand_emb.shape[1]
    events = history.shape[1]
    blocks = 4 * D // DH
    anywhere = pl.BlockSpec(memory_space=pl.ANY)
    count = 2 + len(PIECES) + (2 if O_APART else 1)
    return pl.pallas_call(
        fused_kernel,
        out_shape=pltpu.VMEM(cand_emb.shape, jnp.bfloat16),
        in_specs=[anywhere] * 7,
        out_specs=pl.BlockSpec(memory_space=pltpu.VMEM),
        scratch_shapes=[
            pltpu.SMEM((1,), jnp.int32),
            pltpu.SMEM((1, 1), jnp.int32),
            pltpu.VMEM((1, D), jnp.float32),
            pltpu.VMEM((slots, D), jnp.bfloat16),
            pltpu.VMEM((RING, events, D // RING), jnp.bfloat16),
            pltpu.VMEM((2, RING, D, 2 * D // RING), jnp.bfloat16),
            pltpu.VMEM((RING, D, D // RING), jnp.bfloat16),
            pltpu.VMEM((slots, D), jnp.bfloat16),
            pltpu.VMEM((events, D), jnp.bfloat16),
            pltpu.VMEM((blocks, slots, DH), jnp.bfloat16),
            pltpu.VMEM((blocks // 2, events, DH), jnp.bfloat16),
            pltpu.VMEM((HEADS, slots, DH), jnp.float32),
            pltpu.VMEM((slots, D), jnp.bfloat16),
            pltpu.SemaphoreType.DMA((count,)),
            pltpu.SemaphoreType.DMA((count, 4)),
            pltpu.SemaphoreType.DMA((12,)),
            pltpu.SemaphoreType.DMA((4, 4)),
            pltpu.SemaphoreType.DMA((4, 4)),
            pltpu.SemaphoreType.DMA((8,)),
        ],
        compiler_params=pltpu.CompilerParams(
            collective_id=0, has_side_effects=True, vmem_limit_bytes=56 * 1024 * 1024
        ),
        name="score_fused",
    )(hist_len, tile_counts, history, w_in, w_out, cand_emb, out_gain.reshape(1, D))


def attend_rows(carry, kv_piece, queries, length, score_scale):
    key_count = kv_piece.shape[0]
    values = kv_piece[:, :D].reshape(key_count, HEADS, DH)
    key_heads = kv_piece[:, D:].reshape(key_count, HEADS, DH)
    scores = (
        jnp.einsum("rhe,the->hrt", queries, key_heads, preferred_element_type=jnp.float32)
        * score_scale
    )
    positions = jnp.arange(key_count, dtype=jnp.int32)
    weights = jnp.where(positions[None, None, :] < length, jax.nn.silu(scores), 0.0).astype(
        jnp.bfloat16
    )
    mixed_sum = jnp.einsum("hrt,the->rhe", weights, values, preferred_element_type=jnp.float32)
    return mixed_sum.reshape(carry.shape)


def score_rows(embedded, history, length, w_in, out_gain, w_out):
    score_scale = 1.0 / math.sqrt(DH)
    rows_here = embedded.shape[0]
    normed = layer_norm(embedded.astype(jnp.float32)).astype(jnp.bfloat16)
    initial = jnp.zeros((rows_here, D), jnp.float32)
    own_events = lax.all_to_all(history, "cand", split_axis=0, concat_axis=1, tiled=True)
    hist_normed = layer_norm(own_events.astype(jnp.float32)).astype(jnp.bfloat16)
    stacked = jnp.concatenate([normed, hist_normed], axis=0)
    projected = jax.nn.silu(
        jnp.dot(
            stacked,
            lax.all_gather(w_in, "cand", axis=1, tiled=True),
            preferred_element_type=jnp.float32,
        )
    ).astype(jnp.bfloat16)
    proj_rows = projected[:rows_here]
    hist_proj = projected[rows_here:]
    kv_local = jnp.concatenate([hist_proj[:, D : 2 * D], hist_proj[:, 3 * D :]], axis=1)
    queries = proj_rows[:, 2 * D : 3 * D].reshape(rows_here, HEADS, DH)
    summed = attend_rows(
        initial, lax.all_gather(kv_local, "cand", axis=0, tiled=True), queries, length, score_scale
    )
    gate_part = proj_rows[:, :D].astype(jnp.float32)
    cand_values = proj_rows[:, D : 2 * D].reshape(rows_here, HEADS, DH).astype(jnp.float32)
    cand_keys = proj_rows[:, 3 * D :].reshape(rows_here, HEADS, DH).astype(jnp.float32)
    own_score = jax.nn.silu(jnp.sum(queries.astype(jnp.float32) * cand_keys, axis=-1) * score_scale)
    attn = summed + (own_score[:, :, None] * cand_values).reshape(rows_here, D)
    gated = (layer_norm(attn) * out_gain[None, :] * gate_part).astype(jnp.bfloat16)
    residual = embedded.astype(jnp.float32)
    return (
        residual
        + jnp.dot(
            gated,
            lax.all_gather(w_out, "cand", axis=1, tiled=True),
            preferred_element_type=jnp.float32,
        )
    ).astype(jnp.bfloat16)


def shards(history, hist_len, tile_counts, cand_emb, w_in, out_gain, w_out):
    tile_total = tile_counts[0, 0]
    length = hist_len[0]
    slot_rows = cand_emb[0]
    slot_count = slot_rows.shape[0]
    own_history = history[0]
    scored = score_rows(slot_rows, own_history, length, w_in, out_gain, w_out)
    live = jnp.arange(slot_count, dtype=jnp.int32) < tile_total * TILE
    result = jnp.where(live[:, None], scored, jnp.zeros_like(scored))
    return result[None]


def solution(mesh):
    in_specs = (
        P(("group", "user"), None, "cand"),
        P(("group", "user")),
        P(("group", "user"), "cand"),
        P(("group", "user"), "cand", None),
        P(None, "cand"),
        P(),
        P(None, "cand"),
    )
    out_specs = P(("group", "user"), "cand", None)
    sizes = tuple(mesh.shape[name] for name in ("group", "user", "cand"))
    body = fused_shards if sizes == (2, 2, RING) else shards
    return jax.shard_map(body, mesh=mesh, in_specs=in_specs, out_specs=out_specs, check_vma=False)
```

```python
import functools
import math

import jax
import jax.numpy as jnp
from jax import lax
from jax.experimental import pallas as pl
from jax.experimental.pallas import tpu as pltpu
from jax.sharding import PartitionSpec as P

D = 1024
HEADS = 8
DH = 128
TILE = 128
RING = 8
MESH = pl.DeviceIdType.MESH


def layer_norm(values, scale=1.0):
    center = values - jnp.mean(values, axis=-1, keepdims=True)
    spread = jnp.mean(center * center, axis=-1, keepdims=True)
    return center * (lax.rsqrt(spread + 1e-05) * scale)


def half_silu(half):
    return half + half * jnp.tanh(half)


def cand_of(place):
    high = place // 4
    return (1 - high) * (2 * place) + high * (15 - 2 * place)


def place_of(cand):
    row, column = cand // 2, cand % 2
    return (1 - column) * row + column * (7 - row)


PIECES = (5, 3)
O_APART = 64

KV_ORDER = (0o3111, 0o4336, 0o1443, 0o6664)

PLAN = (
    ('send', 'W1', 0),
    ('send', 'W0', 0),
    ('send', 'O1', 0),
    ('send', 'H0', 0),
    ('nb',),
    ('pc', 'W0', 'own'),
    ('pc', 'W1', 'own'),
    ('recv', 'W1', 0),
    ('send', 'W1', 1),
    ('recv', 'W0', 0),
    ('recv', 'O1', 0),
    ('recv', 'H0', 0),
    ('send', 'H0', 1),
    ('side', 'W1', 0),
    ('full', 'W1', 0),
    ('recv', 'W1', 1),
    ('send', 'W1', 2),
    ('send', 'O1', 1),
    ('pc', 'W1', 0),
    ('recv', 'H0', 1),
    ('send', 'H0', 2),
    ('side', 'W0', 0),
    ('side', 'O1', 0),
    ('full', 'W0', 0),
    ('pc', 'W0', 0),
    ('full', 'O1', 0),
    ('recv', 'W1', 2),
    ('send', 'W1', 3),
    ('send', 'H1', 0),
    ('send', 'W0', 1),
    ('recv', 'O1', 1),
    ('send', 'O1', 2),
    ('recv', 'H0', 2),
    ('send', 'H0', 3),
    ('side', 'W1', 1),
    ('recv', 'W1', 3),
    ('full', 'W1', 1),
    ('pc', 'W1', 1),
    ('recv', 'H1', 0),
    ('send', 'H1', 1),
    ('side', 'W1', 2),
    ('recv', 'W0', 1),
    ('send', 'W0', 2),
    ('side', 'O1', 1),
    ('recv', 'O1', 2),
    ('full', 'W1', 2),
    ('pc', 'W1', 2),
    ('full', 'O1', 1),
    ('recv', 'H0', 3),
    ('hn', 0),
    ('side', 'W1', 3),
    ('ph', 'W0', 0, 0),
    ('ph', 'W1', 0, 0),
    ('recv', 'H1', 1),
    ('send', 'H1', 2),
    ('send', 'O0', 0),
    ('send', 'O1', 3),
    ('full', 'W1', 3),
    ('ph', 'W1', 0, 2),
    ('ph', 'W1', 0, 1),
    ('at', 'near', 'W1', 0),
    ('ph', 'W1', 0, 3),
    ('recv', 'W0', 2),
    ('pc', 'W1', 3),
    ('at', 'far', 'W1', 0),
    ('side', 'W0', 1),
    ('recv', 'H1', 2),
    ('send', 'H1', 3),
    ('send', 'W0', 3),
    ('side', 'O1', 2),
    ('full', 'W0', 1),
    ('ph', 'W0', 0, 1),
    ('pc', 'W0', 1),
    ('full', 'O1', 2),
    ('recv', 'O0', 0),
    ('send', 'O0', 1),
    ('recv', 'O1', 3),
    ('recv', 'H1', 3),
    ('hn', 1),
    ('full', 'O0', 0),
    ('ph', 'W0', 1, 1),
    ('ph', 'W1', 1, 3),
    ('recv', 'W0', 3),
    ('ph', 'W1', 1, 0),
    ('ph', 'W1', 1, 2),
    ('ph', 'W1', 1, 1),
    ('side', 'W0', 2),
    ('side', 'O1', 3),
    ('at', 'far', 'W1', 1),
    ('recv', 'O0', 1),
    ('send', 'O0', 2),
    ('at', 'near', 'W1', 1),
    ('full', 'W0', 2),
    ('full', 'O1', 3),
    ('pc', 'W0', 2),
    ('full', 'O0', 1),
    ('ph', 'W0', 1, 2),
    ('ph', 'W0', 0, 2),
    ('at', 'near', 'W0', 0),
    ('side', 'W0', 3),
    ('ph', 'W0', 1, 0),
    ('at', 'near', 'W0', 1),
    ('recv', 'O0', 2),
    ('send', 'O0', 3),
    ('full', 'W0', 3),
    ('pc', 'W0', 3),
    ('ph', 'W0', 0, 3),
    ('at', 'far', 'W0', 0),
    ('full', 'O0', 2),
    ('ph', 'W0', 1, 3),
    ('at', 'far', 'W0', 1),
    ('ln',),
    ('recv', 'O0', 3),
    ('out', 1),
    ('out', 2),
    ('out', 0),
    ('full', 'O0', 3),
    ('out', 3),
)


def fused_kernel(
    length_hbm, tiles_hbm, hist_ref, w_ref, wo_ref, cand_ref, gain_hbm, out_ref,
    length_ref, tiles_ref, gain_ref, cb, hb, wb, ob, nb, hn, pb, kvb, ab, gb,
    ring_send, ring_recv, side_send, side_recv, core_recv, local_sem,
):
    group = lax.axis_index("group")
    user = lax.axis_index("user")
    me = lax.axis_index("cand")
    place = place_of(me)
    slots = cand_ref.shape[1]
    events = hist_ref.shape[1]

    def shard_at(offset):
        return cand_of((place + offset + RING) % RING)

    core_peer = {"user": 1 - user}
    y_peer = {"group": 1 - group}
    ring_peer = ({"cand": shard_at(1)}, {"cand": shard_at(-1)})

    quarter = D // 4
    half = D // 2

    def w_rows(g, u):
        return (2 * g + u) * quarter

    def o_rows(g, u):
        return u * half + g * (half - O_APART)

    spans = []
    first = 0
    for size in PIECES:
        spans.append((first * (events // 8), size * (events // 8)))
        first += size

    streams = {}
    for j in range(2):
        streams[("W", j)] = (
            w_ref.at[:, pl.ds(j * quarter, quarter)], wb.at[j], w_rows(group, user), quarter
        )
    for e, (start, size) in enumerate(spans):
        streams[("H", e)] = (hist_ref.at[0], hb, start, size)
    streams[("O", 0)] = (wo_ref, ob, user * half + O_APART, half - 2 * O_APART)
    if O_APART:
        streams[("O", 1)] = (wo_ref, ob, o_rows(group, user), O_APART)
    names = list(streams)
    sided = [name for name in names if name[0] != "H"]
    shared = [name for name in sided if name != ("O", 0)]

    def side_rows(name, kind, g, u):
        if name[0] == "W":
            return (w_rows(g, u), w_rows(g, u), w_rows(1 - g, u))[kind], quarter
        if name[1] == 0:
            return u * half + O_APART, half - 2 * O_APART
        return (o_rows(g, u), o_rows(g, u), o_rows(1 - g, u))[kind], O_APART

    CORE, Y, DIAG = 0, 1, 2

    barrier = pltpu.get_barrier_semaphore()
    for peer in (ring_peer[0], ring_peer[1], core_peer, y_peer):
        pl.semaphore_signal(barrier, inc=1, device_id=peer, device_id_type=MESH)

    fetch = pltpu.make_async_copy(cand_ref.at[0], cb, local_sem.at[4])
    fetch.start()
    own = [
        pltpu.make_async_copy(hist_ref.at[0], hb.at[me], local_sem.at[0]),
        pltpu.make_async_copy(wo_ref, ob.at[me], local_sem.at[1]),
    ]
    for j in range(2):
        own.append(
            pltpu.make_async_copy(streams[("W", j)][0], wb.at[j, me], local_sem.at[2 + j])
        )
    small = [
        pltpu.make_async_copy(length_hbm, length_ref, local_sem.at[5]),
        pltpu.make_async_copy(gain_hbm, gain_ref, local_sem.at[6]),
        pltpu.make_async_copy(tiles_hbm, tiles_ref, local_sem.at[7]),
    ]
    for copy in own + small:
        copy.start()
    pl.semaphore_wait(barrier, 4)

    def ring_copy(name, way, step, shard, first):
        source, buffer, start, size = streams[name]
        if step == 3:
            size = size // 2
            start = start + way * size
        rows = pl.ds(start if isinstance(start, int) else pl.multiple_of(start, 16), size)
        spot = buffer.at[shard, rows, :]
        index = names.index(name)
        return pltpu.make_async_remote_copy(
            src_ref=source.at[rows, :] if first else spot,
            dst_ref=spot,
            send_sem=ring_send.at[index],
            recv_sem=ring_recv.at[index, step],
            device_id=ring_peer[way],
            device_id_type=MESH,
        )

    def landed(name, shards, rows):
        return streams[name][1].at[pl.ds(0, shards), pl.ds(0, rows), :]

    def wait_for(sem, spot):
        pltpu.make_async_copy(spot, spot, sem).wait()

    def ring_start(name, step):
        for way in range(2):
            shard = shard_at(-step if way == 0 else step)
            ring_copy(name, way, step, shard, step == 0).start()

    def ring_wait(name, step):
        size = streams[name][3]
        shards = 1 if step == 3 else 2
        wait_for(ring_recv.at[names.index(name), step], landed(name, shards, size))

    def spots(step):
        return (4,) if step == 3 else (-1 - step, step + 1)

    def side_start(name, kind, step):
        start, size = side_rows(name, kind, group, user)
        index = sided.index(name)
        for offset in spots(step):
            spot = streams[name][1].at[
                shard_at(offset), pl.ds(pl.multiple_of(start, 16), size), :
            ]
            pltpu.make_async_remote_copy(
                src_ref=spot, dst_ref=spot,
                send_sem=side_send.at[3 * index + kind],
                recv_sem=(side_recv if kind == Y else core_recv).at[index, step],
                device_id=y_peer if kind == Y else core_peer, device_id_type=MESH,
            ).start()

    def take_ring(name, step):
        ring_wait(name, step)
        if name in shared:
            side_start(name, Y, step)
        if name in sided:
            side_start(name, CORE, step)

    def take_side(name, step):
        rows = side_rows(name, Y, group, user)[1]
        wait_for(side_recv.at[sided.index(name), step], landed(name, len(spots(step)), rows))
        side_start(name, DIAG, step)

    def take_core(name, step):
        rows = side_rows(name, CORE, group, user)[1]
        if name in shared:
            rows = 2 * rows
        wait_for(core_recv.at[sided.index(name), step], landed(name, len(spots(step)), rows))

    def over(step, body):
        if step == "own":
            body(me)
        elif step == 3:
            body(shard_at(4))
        else:
            for way in range(2):
                body(shard_at((1 - 2 * way) * (step + 1)))

    def project_cand(j, shard):
        product = jnp.dot(nb[...], wb[j, shard], preferred_element_type=jnp.float32)
        act = half_silu(product).astype(jnp.bfloat16)
        for i in range(2):
            pb[4 * shard + 2 * j + i] = act[:, i * DH : (i + 1) * DH]

    def norm_hist(e):
        length = length_ref[0]
        start, size = spans[e]
        chunk = 128

        @pl.loop(0, size // chunk, unroll=True)
        def _(i):
            first = pl.multiple_of(start + i * chunk, chunk)
            rows = pl.ds(first, chunk)
            whole = jnp.concatenate([hb[c, rows, :] for c in range(RING)], axis=1)
            event = lax.broadcasted_iota(jnp.int32, (chunk, 1), 0) + first
            kept = jnp.where(event < length, 0.5, 0.0)
            hn[rows, :] = layer_norm(whole.astype(jnp.float32), kept).astype(jnp.bfloat16)

    high = place // 4
    low = (1 - high) * place + high * (RING - 1 - place)
    digit = (1 + 7 * (low % 2)) * (1 + 63 * (low // 2))

    def project_hist(j, e, turn):
        start, size = (0, events) if e is None else spans[e]
        owner = (KV_ORDER[turn] // digit) % 8
        shard = cand_of((1 - high) * owner + high * (RING - 1 - owner))
        first = 4 * shard - 8 - 8 * (shard // 4) + 2 * j
        rows = pl.ds(start, size)
        product = jnp.dot(hn[rows, :], wb[j, shard], preferred_element_type=jnp.float32)
        act = half_silu(product).astype(jnp.bfloat16)
        for i in range(2):
            kvb[first + i, rows, :] = act[:, i * DH : (i + 1) * DH]

    half_scale = 0.5 / math.sqrt(DH)
    near = (HEADS // 2) * (me % 2)

    def attend(first, e, fresh):
        rows = pl.ds(*((0, events) if e is None else spans[e]))
        for i in range(2):
            head = first + i
            query = pb[2 * HEADS + head]
            scores = lax.dot_general(
                query, kvb[HEADS + head, rows, :], (((1,), (1,)), ((), ())),
                preferred_element_type=jnp.float32,
            )
            weights = half_silu(scores * half_scale).astype(jnp.bfloat16)
            mixed = jnp.dot(weights, kvb[head, rows, :], preferred_element_type=jnp.float32)
            if fresh:
                own_sum = jnp.sum(
                    query.astype(jnp.float32) * pb[3 * HEADS + head].astype(jnp.float32),
                    axis=-1, keepdims=True,
                )
                own_weight = half_silu(own_sum * half_scale)
                ab[head] = mixed + own_weight * pb[HEADS + head].astype(jnp.float32)
            else:
                ab[head] += mixed

    def gate_rows():
        chunk = 128

        @pl.loop(0, slots // chunk, unroll=True)
        def _(i):
            rows = pl.ds(pl.multiple_of(i * chunk, chunk), chunk)
            attn = jnp.concatenate([ab[h, rows, :] for h in range(HEADS)], axis=1)
            gate = jnp.concatenate([pb[h, rows, :] for h in range(HEADS)], axis=1)
            gb[rows, :] = (
                layer_norm(attn) * gain_ref[...] * gate.astype(jnp.float32)
            ).astype(jnp.bfloat16)

    def project_out(step):
        shards = (me, shard_at(4)) if step == 3 else (shard_at(-1 - step), shard_at(step + 1))
        pair = jnp.concatenate([ob[shard] for shard in shards], axis=1)
        added = jnp.dot(gb[...], pair, preferred_element_type=jnp.float32)
        slot = lax.broadcasted_iota(jnp.int32, (slots, 1), 0)
        live = slot < tiles_ref[0, 0] * TILE
        for i, shard in enumerate(shards):
            columns = pl.ds(pl.multiple_of(shard * DH, DH), DH)
            result = cb[:, columns].astype(jnp.float32) + added[:, i * DH : (i + 1) * DH]
            out_ref[0, :, columns] = jnp.where(live, result, 0.0).astype(jnp.bfloat16)

    seen = set()
    for what, *rest in PLAN:
        if what in ("send", "recv", "side", "full"):
            act = {"send": ring_start, "recv": take_ring, "side": take_side, "full": take_core}
            act[what]((rest[0][0], int(rest[0][1])), rest[1])
        elif what == "nb":
            fetch.wait()
            nb[...] = layer_norm(cb[...].astype(jnp.float32), 0.5).astype(jnp.bfloat16)
            for copy in own + small:
                copy.wait()
        elif what == "pc":
            over(rest[1], functools.partial(project_cand, int(rest[0][1])))
        elif what == "hn":
            norm_hist(rest[0])
        elif what == "ph":
            project_hist(int(rest[0][1]), rest[1], rest[2])
        elif what == "at":
            j = int(rest[1][1])
            first = (near if rest[0] == "near" else HEADS // 2 - near) + 2 * j
            attend(first, rest[2], (rest[0], j) not in seen)
            seen.add((rest[0], j))
        elif what == "ln":
            gate_rows()
        else:
            project_out(rest[0])

    for name in names:
        wait_for(ring_send.at[names.index(name)], landed(name, RING - 1, streams[name][3]))
    for name in sided:
        for kind in (CORE, Y, DIAG) if name in shared else (CORE,):
            rows = side_rows(name, kind, group, user)[1]
            wait_for(side_send.at[3 * sided.index(name) + kind], landed(name, RING - 1, rows))


def fused_shards(history, hist_len, tile_counts, cand_emb, w_in, out_gain, w_out):
    slots = cand_emb.shape[1]
    events = history.shape[1]
    blocks = 4 * D // DH
    anywhere = pl.BlockSpec(memory_space=pl.ANY)
    count = 2 + len(PIECES) + (2 if O_APART else 1)
    return pl.pallas_call(
        fused_kernel,
        out_shape=pltpu.VMEM(cand_emb.shape, jnp.bfloat16),
        in_specs=[anywhere] * 7,
        out_specs=pl.BlockSpec(memory_space=pltpu.VMEM),
        scratch_shapes=[
            pltpu.SMEM((1,), jnp.int32),
            pltpu.SMEM((1, 1), jnp.int32),
            pltpu.VMEM((1, D), jnp.float32),
            pltpu.VMEM((slots, D), jnp.bfloat16),
            pltpu.VMEM((RING, events, D // RING), jnp.bfloat16),
            pltpu.VMEM((2, RING, D, 2 * D // RING), jnp.bfloat16),
            pltpu.VMEM((RING, D, D // RING), jnp.bfloat16),
            pltpu.VMEM((slots, D), jnp.bfloat16),
            pltpu.VMEM((events, D), jnp.bfloat16),
            pltpu.VMEM((blocks, slots, DH), jnp.bfloat16),
            pltpu.VMEM((blocks // 2, events, DH), jnp.bfloat16),
            pltpu.VMEM((HEADS, slots, DH), jnp.float32),
            pltpu.VMEM((slots, D), jnp.bfloat16),
            pltpu.SemaphoreType.DMA((count,)),
            pltpu.SemaphoreType.DMA((count, 4)),
            pltpu.SemaphoreType.DMA((12,)),
            pltpu.SemaphoreType.DMA((4, 4)),
            pltpu.SemaphoreType.DMA((4, 4)),
            pltpu.SemaphoreType.DMA((8,)),
        ],
        compiler_params=pltpu.CompilerParams(
            collective_id=0, has_side_effects=True, vmem_limit_bytes=56 * 1024 * 1024
        ),
        name="score_fused",
    )(hist_len, tile_counts, history, w_in, w_out, cand_emb, out_gain.reshape(1, D))


def attend_rows(carry, kv_piece, queries, length, score_scale):
    key_count = kv_piece.shape[0]
    values = kv_piece[:, :D].reshape(key_count, HEADS, DH)
    key_heads = kv_piece[:, D:].reshape(key_count, HEADS, DH)
    scores = (
        jnp.einsum("rhe,the->hrt", queries, key_heads, preferred_element_type=jnp.float32)
        * score_scale
    )
    positions = jnp.arange(key_count, dtype=jnp.int32)
    weights = jnp.where(positions[None, None, :] < length, jax.nn.silu(scores), 0.0).astype(
        jnp.bfloat16
    )
    mixed_sum = jnp.einsum("hrt,the->rhe", weights, values, preferred_element_type=jnp.float32)
    return mixed_sum.reshape(carry.shape)


def score_rows(embedded, history, length, w_in, out_gain, w_out):
    score_scale = 1.0 / math.sqrt(DH)
    rows_here = embedded.shape[0]
    normed = layer_norm(embedded.astype(jnp.float32)).astype(jnp.bfloat16)
    initial = jnp.zeros((rows_here, D), jnp.float32)
    own_events = lax.all_to_all(history, "cand", split_axis=0, concat_axis=1, tiled=True)
    hist_normed = layer_norm(own_events.astype(jnp.float32)).astype(jnp.bfloat16)
    stacked = jnp.concatenate([normed, hist_normed], axis=0)
    projected = jax.nn.silu(
        jnp.dot(
            stacked,
            lax.all_gather(w_in, "cand", axis=1, tiled=True),
            preferred_element_type=jnp.float32,
        )
    ).astype(jnp.bfloat16)
    proj_rows = projected[:rows_here]
    hist_proj = projected[rows_here:]
    kv_local = jnp.concatenate([hist_proj[:, D : 2 * D], hist_proj[:, 3 * D :]], axis=1)
    queries = proj_rows[:, 2 * D : 3 * D].reshape(rows_here, HEADS, DH)
    summed = attend_rows(
        initial, lax.all_gather(kv_local, "cand", axis=0, tiled=True), queries, length, score_scale
    )
    gate_part = proj_rows[:, :D].astype(jnp.float32)
    cand_values = proj_rows[:, D : 2 * D].reshape(rows_here, HEADS, DH).astype(jnp.float32)
    cand_keys = proj_rows[:, 3 * D :].reshape(rows_here, HEADS, DH).astype(jnp.float32)
    own_score = jax.nn.silu(jnp.sum(queries.astype(jnp.float32) * cand_keys, axis=-1) * score_scale)
    attn = summed + (own_score[:, :, None] * cand_values).reshape(rows_here, D)
    gated = (layer_norm(attn) * out_gain[None, :] * gate_part).astype(jnp.bfloat16)
    residual = embedded.astype(jnp.float32)
    return (
        residual
        + jnp.dot(
            gated,
            lax.all_gather(w_out, "cand", axis=1, tiled=True),
            preferred_element_type=jnp.float32,
        )
    ).astype(jnp.bfloat16)


def shards(history, hist_len, tile_counts, cand_emb, w_in, out_gain, w_out):
    tile_total = tile_counts[0, 0]
    length = hist_len[0]
    slot_rows = cand_emb[0]
    slot_count = slot_rows.shape[0]
    own_history = history[0]
    scored = score_rows(slot_rows, own_history, length, w_in, out_gain, w_out)
    live = jnp.arange(slot_count, dtype=jnp.int32) < tile_total * TILE
    result = jnp.where(live[:, None], scored, jnp.zeros_like(scored))
    return result[None]


def solution(mesh):
    in_specs = (
        P(("group", "user"), None, "cand"),
        P(("group", "user")),
        P(("group", "user"), "cand"),
        P(("group", "user"), "cand", None),
        P(None, "cand"),
        P(),
        P(None, "cand"),
    )
    out_specs = P(("group", "user"), "cand", None)
    sizes = tuple(mesh.shape[name] for name in ("group", "user", "cand"))
    body = fused_shards if sizes == (2, 2, RING) else shards
    return jax.shard_map(body, mesh=mesh, in_specs=in_specs, out_specs=out_specs, check_vma=False)
```
